32 devices in a mesh: chan: 16 (over z, y, core), slot: 2 (over x).
Axes of the slice: x: 2, y: 2, z: 4, core: 2. Of those that a mesh axis runs over, the one named last changes fastest.
Arguments:
- measured_real: float32 [2, 16, 1770], P('slot', 'chan'), may hold values from -60 to 60
- measured_imaginary: float32 [2, 16, 1770], P('slot', 'chan'), may hold values from -60 to 60
- measured_weight: float32 [2, 16, 1770], P('slot', 'chan'), may hold values from 0.3 to 3
- baseline_vectors: float32 [2, 3, 1770], P('slot'), may hold values from -120 to 120
- antenna_pairs: int32 [2, 1770], replicated, may hold values from 0 to 59, as said below
- directions: float32 [3, 200], replicated, may hold values from -0.12 to 0.12
- direction_flux: float32 [16, 200], P('chan'), may hold values from 0.2 to 2
- channel_frequency: float32 [16], P('chan'), may hold values from 1.1 to 1.9
- electron_content_start: float32 [2, 60, 200], P('slot'), may hold values from -6 to 6
- pierce_station_direction: int32 [2, 12000], P('slot'), may hold values from 0 to 11999, each once within a row
- eigen_basis: float32 [12000, 2048], P('chan'), may hold values from -0.0546875 to 0.0546875
- eigen_weight: float32 [2048], replicated, may hold values from 0.1 to 1
Outputs:
- tec_final: float32 [2, 60, 200], P('slot')
- coefficients: float32 [2, 2048], P('slot')
- final_residual_real: float32 [2, 16, 1770], P('slot', 'chan')
- final_residual_imaginary: float32 [2, 16, 1770], P('slot', 'chan')
The draws below stay inside these ranges and needn't reach their ends.
Inputs may be any that keep to these rules, and one draw needn't show every extreme that they name: `antenna_pairs`: each column is a pair of two different stations, and the 1770 columns hold every unordered pair of stations exactly once. `pierce_station_direction`: each row names every station-direction pair exactly once.
All inputs are finite; a program needn't handle non-finite values.
Results may differ from the reference program's by a relative error of at most 0.00018.
Values sent between devices are 32-bit elements; how exact they have to be, the bound alone decides.
A program may use at most 64 MiB of HBM per device.

```python
import math
import jax
import jax.numpy as jnp
from jax import lax

S = 60
D = 200
K = 2048
ITERS = 4
STATION_PAIRS = 1770
P_SIZE = 12000
TIME_SLOTS = 2
FREQ_CHANNELS = 16


def draw_antenna_pairs(key, part):
    first_list, second_list = jnp.triu_indices(S, 1)
    key_permute, key_reverse = jax.random.split(jax.random.fold_in(key, 11))
    sorted_index = jax.random.permutation(key_permute, STATION_PAIRS)
    reversed_pairs = jax.random.randint(key_reverse, (STATION_PAIRS,), 0, 2)
    first_list = first_list[sorted_index]
    second_list = second_list[sorted_index]
    lower = jnp.where(reversed_pairs == 1, second_list, first_list)
    upper = jnp.where(reversed_pairs == 1, first_list, second_list)
    return jnp.stack([lower, upper]).astype(jnp.int32)


def block_levels(own_key, shape, cuts, low, top_value):
    factor_of, own = 1.0, jax.random.fold_in(own_key, 6)
    for dim, shards_of in cuts:
        draws = jnp.exp(jax.random.uniform(jax.random.fold_in(own, dim), (shards_of,), jnp.float32, low / len(cuts), top_value / len(cuts)))
        factor_of = factor_of * jnp.repeat(draws, shape[dim] // shards_of).reshape([-1 if axis == dim else 1 for axis in range(len(shape))])
    return factor_of


def gaussian(key, dims, width, reach, shards=(), held_as=jnp.bfloat16):
    array = width * jax.random.normal(key, dims, jnp.float32)
    if shards:
        array = array * block_levels(key, dims, shards, -0.22, 0.18)
    return jnp.clip(array, -reach, reach).astype(held_as)


def setup_inputs(seed: int = 0) -> dict:
    key_list = jax.random.split(jax.random.key(seed), 13)
    measured_real = gaussian(key_list[0], (TIME_SLOTS, FREQ_CHANNELS, STATION_PAIRS), 10.0, 60.0, ((0, 2), (1, 16)), jnp.float32)
    measured_imaginary = gaussian(key_list[1], (TIME_SLOTS, FREQ_CHANNELS, STATION_PAIRS), 10.0, 60.0, ((0, 2), (1, 16)), jnp.float32)
    measured_weight = jnp.clip(jnp.exp(math.log(3.0) - 2.3025851 * jax.random.uniform(key_list[2], (TIME_SLOTS, FREQ_CHANNELS, STATION_PAIRS), jnp.float32) ** block_levels(key_list[2], (TIME_SLOTS, FREQ_CHANNELS, STATION_PAIRS), ((0, 2), (1, 16)), -0.2, 0.2)), 0.3, 3.0)
    baseline_vectors = gaussian(key_list[3], (TIME_SLOTS, 3, STATION_PAIRS), 20.0, 120.0, ((0, 2),), jnp.float32)
    antenna_pairs = draw_antenna_pairs(jax.random.fold_in(key_list[12], 71), 0)
    directions = gaussian(key_list[5], (3, D), 0.02, 0.12, (), jnp.float32)
    direction_flux = jnp.clip(jnp.exp(math.log(2.0) - 2.3025851 * jax.random.uniform(key_list[6], (FREQ_CHANNELS, D), jnp.float32) ** block_levels(key_list[6], (FREQ_CHANNELS, D), ((0, 16),), -0.2, 0.2)), 0.2, 2.0)
    channel_frequency = jnp.clip(1.1 + 0.79999995 * jax.random.uniform(key_list[7], (FREQ_CHANNELS,), jnp.float32) ** block_levels(key_list[7], (FREQ_CHANNELS,), ((0, 16),), -0.2, 0.2), 1.1, 1.9)
    electron_content_start = gaussian(key_list[8], (TIME_SLOTS, S, D), 1.0, 6.0, ((0, 2),), jnp.float32)
    pierce_station_direction = jax.vmap(lambda own: jax.random.permutation(own, P_SIZE))(jax.random.split(key_list[9], TIME_SLOTS)).reshape((TIME_SLOTS, P_SIZE)).astype(jnp.int32)
    eigen_basis = gaussian(key_list[10], (P_SIZE, K), P_SIZE ** -0.5, 0.0546875, ((0, 16),), jnp.float32)
    eigen_weight = jnp.clip(jnp.exp(jax.random.uniform(key_list[11], (K,), jnp.float32, math.log(0.1), math.log(1.0))), 0.1, 1.0)
    return dict(measured_real=measured_real, measured_imaginary=measured_imaginary, measured_weight=measured_weight, baseline_vectors=baseline_vectors, antenna_pairs=antenna_pairs, directions=directions, direction_flux=direction_flux, channel_frequency=channel_frequency, electron_content_start=electron_content_start, pierce_station_direction=pierce_station_direction, eigen_basis=eigen_basis, eigen_weight=eigen_weight)


HIGHEST = lax.Precision.HIGHEST
TEC_PHASE = -0.8448
SMOOTHING = 0.5
TWO_PI = 6.283185307179586


def station_polarity(antenna_pairs):
    station_list = jnp.arange(S, dtype=jnp.int32)[:, None]
    first_match = (antenna_pairs[0][None, :] == station_list).astype(jnp.float32)
    second_match = (antenna_pairs[1][None, :] == station_list).astype(jnp.float32)
    return first_match - second_match, first_match + second_match


def pair_terms(vis_real, vis_imag, weights, coords, frequency, fluxes, tec_slot, signed_terms, directions):
    geometry = (TWO_PI * frequency) * jnp.dot(coords.T, directions, precision=HIGHEST)
    station_phase = (TEC_PHASE / frequency) * tec_slot
    phases = geometry + jnp.dot(signed_terms.T, station_phase, precision=HIGHEST)
    model_real = fluxes[None, :] * jnp.cos(phases)
    model_imag = fluxes[None, :] * jnp.sin(phases)
    leftover_real = vis_real - jnp.sum(model_real, axis=1)
    leftover_imaginary = vis_imag - jnp.sum(model_imag, axis=1)
    projected = weights[:, None] * (model_real * leftover_imaginary[:, None] - model_imag * leftover_real[:, None])
    numerator = (TEC_PHASE / frequency) * jnp.dot(signed_terms, projected, precision=HIGHEST)
    return numerator, leftover_real, leftover_imaginary


def reference(measured_real, measured_imaginary, measured_weight, baseline_vectors, antenna_pairs, directions, direction_flux, channel_frequency, electron_content_start, pierce_station_direction, eigen_basis, eigen_weight):
    signed_terms, station_touches = station_polarity(antenna_pairs)
    tec_scale = TEC_PHASE / channel_frequency
    station_weight = jnp.einsum('sb,tfb->tfs', station_touches, measured_weight, precision=HIGHEST)
    denominator = jnp.einsum('tfs,fd->tsd', station_weight * (tec_scale * tec_scale)[None, :, None], direction_flux * direction_flux, precision=HIGHEST)
    slot_count = electron_content_start.shape[0]
    denom_flat = denominator.reshape(slot_count, -1)
    tec_flat = electron_content_start.reshape(slot_count, -1)
    slot_rows = jnp.arange(slot_count, dtype=jnp.int32)[:, None]
    position = jnp.arange(slot_count, dtype=jnp.int32)
    neighbours = (position > 0).astype(jnp.float32) + (position < slot_count - 1).astype(jnp.float32)
    smooth = None
    leftover_real = None
    leftover_imaginary = None
    for iteration in range(ITERS):
        current = tec_flat

        def slot_terms(slot_index):
            tec_slot = current[slot_index].reshape(S, D)

            def channel_step(running, channel):
                numerator, part_real, part_imag = pair_terms(measured_real[slot_index, channel], measured_imaginary[slot_index, channel], measured_weight[slot_index, channel], baseline_vectors[slot_index], channel_frequency[channel], direction_flux[channel], tec_slot, signed_terms, directions)
                return running + numerator, (part_real, part_imag)

            running, (part_real, part_imag) = lax.scan(channel_step, jnp.zeros((S, D), jnp.float32), jnp.arange(FREQ_CHANNELS, dtype=jnp.int32))
            return running, part_real, part_imag

        numerator, leftover_real, leftover_imaginary = lax.map(slot_terms, jnp.arange(slot_count, dtype=jnp.int32))
        update = current + numerator.reshape(slot_count, -1) / denom_flat
        target = jnp.take_along_axis(update, pierce_station_direction, axis=1)
        raw = eigen_weight[None, :] * jnp.dot(target, eigen_basis, precision=HIGHEST)
        padded = jnp.pad(raw, ((1, 1), (0, 0)))
        smooth = (raw + SMOOTHING * (padded[:-2] + padded[2:])) / (1.0 + SMOOTHING * neighbours)[:, None]
        screen = jnp.dot(smooth, eigen_basis.T, precision=HIGHEST)
        tec_flat = jnp.zeros_like(screen).at[slot_rows, pierce_station_direction].set(screen)
    return tec_flat.reshape(slot_count, S, D), smooth, leftover_real, leftover_imaginary
```

```python
import functools

import jax
import jax.numpy as jnp
from jax import lax
from jax.experimental import pallas as pl
from jax.experimental.pallas import tpu as pltpu
from jax.sharding import PartitionSpec as P

ITERS = 4
TEC_PHASE = -0.8448
SMOOTHING = 0.5
TWO_PI = 6.283185307179586
LANES = 128
TILE = 256

COS_TERMS = ()
SIN_TERMS = ()


def _fit():
    import numpy as np

    nodes = 4000
    theta = np.pi * (np.arange(nodes) + 0.5) / nodes
    u = 0.125 * (1.0 + np.cos(theta))
    r = np.sqrt(u)
    out = []
    for values in (np.cos(2 * np.pi * r), np.sin(2 * np.pi * r) / r):
        cheb = np.polynomial.chebyshev.Chebyshev.fit(u, values, 7, domain=[0.0, 0.25])
        coefs = cheb.convert(kind=np.polynomial.Polynomial).coef
        out.append(tuple(float(np.float32(c)) for c in coefs))
    return out


COS_TERMS, SIN_TERMS = _fit()


def round_up(value, unit):
    return -(-value // unit) * unit


def horner(terms, u):
    acc = jnp.full_like(u, terms[-1])
    for term in terms[-2::-1]:
        acc = acc * u + term
    return acc


def split3(x):
    hi = x.astype(jnp.bfloat16)
    rest = x - hi.astype(jnp.float32)
    mid = rest.astype(jnp.bfloat16)
    low = (rest - mid.astype(jnp.float32)).astype(jnp.bfloat16)
    return hi, mid, low


def dot32(a, b, ca, cb):
    return lax.dot_general(a, b, (((ca,), (cb,)), ((), ())), preferred_element_type=jnp.float32)


def solve_kernel(
    geo,
    vr_ref, vi_ref, w_ref, bv_ref, pairs_ref, cols_ref, flux_ref, freq_ref, tec0_ref,
    smap_ref, dmap_ref, basis_ref, ew_ref,
    tec_out, coef_out, rr_out, ri_out,
    visr, visi, wt, geom, sign3, sgn, fluxb, phase, mre, mim, phi, plo,
    tec, tec3, acc, den, basis, ones3, oned, onedf, target, place,
    stage, abuf, bbuf, craw, cbuf, dbuf, ebuf, fbuf,
    basis_sem, send_sem, recv_sem, csend, crecv,
):
    n, slots, tiles, base_n, srcs, drows, sp, dp, cr, rows, rpad, kk, cw = geo
    me = lax.axis_index("chan")
    slot = lax.axis_index("slot")
    offs = sorted({1 % slots, (slots - 1) % slots} - {0})

    def peer(k):
        return lax.rem(me + k, n)

    whole8 = rows // 8 * 8
    load = pltpu.make_async_copy(basis_ref, basis, basis_sem)
    load.start()

    barrier = pltpu.get_barrier_semaphore()

    def greet(k, c):
        pl.semaphore_signal(
            barrier, inc=1, device_id={"chan": peer(k), "slot": slot},
            device_id_type=pl.DeviceIdType.MESH,
        )
        return c

    lax.fori_loop(1, n, greet, 0)
    for off in offs:

        def greet_far(k, c, off=off):
            pl.semaphore_signal(
                barrier, inc=1,
                device_id={"chan": peer(k), "slot": lax.rem(slot + off, slots)},
                device_id_type=pl.DeviceIdType.MESH,
            )
            return c

        lax.fori_loop(0, n, greet_far, 0)

    freq = freq_ref[...]
    scale = TEC_PHASE / freq
    turn_scale = (TEC_PHASE / TWO_PI) / freq
    fluxb[...] = jnp.broadcast_to(cols_ref[:, 0:1], (drows, TILE))
    station = lax.broadcasted_iota(jnp.int32, (sp, TILE), 0)
    weight_sum = jnp.zeros((sp, 1), jnp.float32)
    for j in range(tiles):
        lo = j * TILE
        width = min(TILE, base_n - lo)
        for dst, src in ((visr, vr_ref[0]), (visi, vi_ref[0]), (wt, w_ref[0])):
            if width < TILE:
                dst[j] = jnp.zeros((1, TILE), jnp.float32)
            dst[j, :, 0:width] = src[:, lo : lo + width]
        pairs = pairs_ref[:, lo : lo + TILE]
        first = (pairs[0:1, :] == station).astype(jnp.float32)
        second = (pairs[1:2, :] == station).astype(jnp.float32)
        polarity = first - second
        weight_sum = weight_sum + jnp.sum((first + second) * wt[j], axis=1, keepdims=True)
        packed = polarity.astype(jnp.bfloat16)
        sgn[j] = packed
        for part in range(3):
            sign3[j, part * sp : (part + 1) * sp, :] = packed

    def split_out(value):
        for j in range(n):
            top, left = (j // (dp // LANES)) * cr, (j % (dp // LANES)) * LANES
            stage[j] = value[top : top + cr, left : left + LANES]

    def scatter_start(phase_id, dst):
        def one(k, c):
            to = peer(k)
            pltpu.make_async_remote_copy(
                src_ref=stage.at[to], dst_ref=dst.at[me],
                send_sem=send_sem.at[phase_id, k], recv_sem=recv_sem.at[phase_id, me],
                device_id={"chan": to, "slot": slot}, device_id_type=pl.DeviceIdType.MESH,
            ).start()
            return c

        lax.fori_loop(1, n, one, 0)

    def gather_start(phase_id, dst):
        def one(k, c):
            pltpu.make_async_remote_copy(
                src_ref=dst.at[me], dst_ref=dst.at[me],
                send_sem=send_sem.at[phase_id, k], recv_sem=recv_sem.at[phase_id, me],
                device_id={"chan": peer(k), "slot": slot},
                device_id_type=pl.DeviceIdType.MESH,
            ).start()
            return c

        lax.fori_loop(1, n, one, 0)

    def finish(phase_id, dst):
        def one(k, c):
            src = peer(k)
            pltpu.make_async_remote_copy(
                src_ref=dst.at[src], dst_ref=dst.at[src],
                send_sem=send_sem.at[phase_id, k], recv_sem=recv_sem.at[phase_id, src],
                device_id={"chan": src, "slot": slot}, device_id_type=pl.DeviceIdType.MESH,
            ).wait()
            return c

        lax.fori_loop(1, n, one, 0)

    def total(buf):
        value = buf[0]
        for j in range(1, n):
            value = value + buf[j]
        return value

    def join(buf, out):
        for j in range(n):
            top, left = (j // (dp // LANES)) * cr, (j % (dp // LANES)) * LANES
            out[top : top + cr, left : left + LANES] = buf[j]

    tec[...] = jnp.zeros((sp, dp), jnp.float32)
    tec[0 : tec0_ref.shape[1], 0:srcs] = tec0_ref[0]
    acc[...] = jnp.zeros((sp, dp), jnp.float32)
    acc[0:1, 0:srcs] = flux_ref[...]
    flux_row = acc[0:1, :]
    part_den = (weight_sum * (scale * scale)) * (flux_row * flux_row)
    for j in range(n):
        top, left = (j // (dp // LANES)) * cr, (j % (dp // LANES)) * LANES
        fbuf[j] = tec[top : top + cr, left : left + LANES]
    split_out(part_den)
    ebuf[me] = stage[me]

    pl.semaphore_wait(barrier, (n - 1) + n * len(offs))
    scatter_start(4, ebuf)

    for j in range(tiles):
        coords = bv_ref[0][:, j * TILE : min((j + 1) * TILE, base_n)]
        width = coords.shape[1]
        value = (
            cols_ref[:, 1:2] * coords[0:1, :]
            + cols_ref[:, 2:3] * coords[1:2, :]
            + cols_ref[:, 3:4] * coords[2:3, :]
        ) * freq
        if width < TILE:
            geom[j] = jnp.zeros((drows, TILE), jnp.float32)
        geom[j, :, 0:width] = value

    lane_s = lax.broadcasted_iota(jnp.int32, (rpad, sp), 1)
    hot_s = (smap_ref[...] == lane_s).astype(jnp.float32)
    for part in range(3):
        ones3[:, part * sp : (part + 1) * sp] = hot_s.astype(jnp.bfloat16)
    lane_d = lax.broadcasted_iota(jnp.int32, (rpad, dp), 1)
    hot_d = (dmap_ref[...] == lane_d).astype(jnp.float32)
    onedf[...] = hot_d
    oned[...] = hot_d.astype(jnp.bfloat16)

    finish(4, ebuf)
    den_sum = total(ebuf)
    den[...] = jnp.where(den_sum == 0.0, 1.0, den_sum)
    load.wait()

    last = slots - 1
    neighbours = jnp.where(slot > 0, 1.0, 0.0) + jnp.where(slot < last, 1.0, 0.0)

    def iteration(it, carry):
        par = lax.rem(it, 2)
        join(fbuf, tec)
        turned = (tec[...] * turn_scale).T
        for part, piece in enumerate(split3(turned)):
            tec3[:, part * sp : (part + 1) * sp] = piece
        acc[...] = jnp.zeros((sp, dp), jnp.float32)

        def pair_tile(j, c):
            phase[...] = dot32(tec3[0:drows, :], sign3[j], 1, 0) + geom[j]
            sum_re = jnp.zeros((8, TILE), jnp.float32)
            sum_im = jnp.zeros((8, TILE), jnp.float32)
            for top in range(0, drows, 16):
                t = phase[top : top + 16, :]
                r = t - jnp.round(t)
                u = r * r
                flux = fluxb[top : top + 16, :]
                re = horner(COS_TERMS, u) * flux
                im = horner(SIN_TERMS, u) * (r * flux)
                mre[top : top + 16, :] = re
                mim[top : top + 16, :] = im
                sum_re = sum_re + re[0:8] + re[8:16]
                sum_im = sum_im + im[0:8] + im[8:16]
            left_re = visr[j] - jnp.sum(sum_re, axis=0, keepdims=True)
            left_im = visi[j] - jnp.sum(sum_im, axis=0, keepdims=True)
            rr_out[j] = left_re
            ri_out[j] = left_im
            wre = wt[j] * left_re
            wim = wt[j] * left_im
            for top in range(0, drows, 16):
                p = mre[top : top + 16, :] * wim - mim[top : top + 16, :] * wre
                hi = p.astype(jnp.bfloat16)
                phi[top : top + 16, :] = hi
                plo[top : top + 16, :] = (p - hi.astype(jnp.float32)).astype(jnp.bfloat16)
            acc[:, 0:drows] += dot32(sgn[j], phi[...], 1, 1) + dot32(sgn[j], plo[...], 1, 1)
            return c

        lax.fori_loop(0, tiles, pair_tile, 0)

        split_out(acc[...] * scale)
        abuf[me] = stage[me]
        scatter_start(0, abuf)
        finish(0, abuf)
        bbuf[me] = fbuf[me] + total(abuf) / den[...]
        gather_start(1, bbuf)
        finish(1, bbuf)
        join(bbuf, acc)

        field = jnp.concatenate([x for x in split3(acc[...])], axis=0)
        picked = dot32(ones3[...], field, 1, 0) * onedf[...]
        target[...] = jnp.broadcast_to(jnp.sum(picked, axis=1, keepdims=True), (rpad, LANES))

        def raw_step(i, sums):
            at = pl.ds(pl.multiple_of(i * 8, 8), 8)
            t = target[at, :]
            return tuple(
                s + basis[at, q * LANES : (q + 1) * LANES] * t for q, s in enumerate(sums)
            )

        zero = jnp.zeros((8, LANES), jnp.float32)
        sums = lax.fori_loop(0, rows // 8, raw_step, tuple(zero for _ in range(kk // LANES)))
        row = jnp.concatenate([jnp.sum(s, axis=0, keepdims=True) for s in sums], axis=1)
        if whole8 < rows:
            rest = target[whole8:rows, 0:1] * basis[whole8:rows, :]
            row = row + jnp.sum(rest, axis=0, keepdims=True)
        row = row * ew_ref[...]
        for j in range(n):
            craw[j] = row[:, j * cw : (j + 1) * cw]
        cbuf[par, 0, me] = craw[me]

        def c_copy(g, off, k):
            to = peer(k)
            return pltpu.make_async_remote_copy(
                src_ref=craw.at[to], dst_ref=cbuf.at[par, g, me],
                send_sem=csend.at[g, k], recv_sem=crecv.at[par, g, me],
                device_id={"chan": to, "slot": lax.rem(slot + off, slots)},
                device_id_type=pl.DeviceIdType.MESH,
            )

        def c_wait(g, off, k):
            src = peer(k)
            pltpu.make_async_remote_copy(
                src_ref=craw.at[src], dst_ref=cbuf.at[par, g, src],
                send_sem=csend.at[g, k], recv_sem=crecv.at[par, g, src],
                device_id={"chan": src, "slot": lax.rem(slot + off, slots)},
                device_id_type=pl.DeviceIdType.MESH,
            ).wait()

        groups = [0] + offs
        for g, off in enumerate(groups):

            def start_one(k, c, g=g, off=off):
                c_copy(g, off, k).start()
                return c

            lax.fori_loop(1 if off == 0 else 0, n, start_one, 0)
        for g, off in enumerate(groups):

            def wait_one(k, c, g=g, off=off):
                c_wait(g, off, k)
                return c

            lax.fori_loop(1 if off == 0 else 0, n, wait_one, 0)
        smooth = total(cbuf.at[par, 0])
        for g, off in enumerate(groups):
            if off:
                source = lax.rem(slot - off + slots, slots)
                near = jnp.abs(source - slot) == 1
                smooth = smooth + total(cbuf.at[par, g]) * jnp.where(near, SMOOTHING, 0.0)
        dbuf[me] = smooth / (1.0 + SMOOTHING * neighbours)
        gather_start(2, dbuf)
        finish(2, dbuf)
        coef = jnp.concatenate([dbuf[j] for j in range(n)], axis=1)
        coef_out[...] = coef
        wide = [
            jnp.broadcast_to(coef[:, q * LANES : (q + 1) * LANES], (8, LANES))
            for q in range(kk // LANES)
        ]

        def screen_step(i, c):
            at = pl.ds(pl.multiple_of(i * 8, 8), 8)
            value = basis[at, 0:LANES] * wide[0]
            for q in range(1, kk // LANES):
                value = value + basis[at, q * LANES : (q + 1) * LANES] * wide[q]
            target[at, :] = value
            return c

        lax.fori_loop(0, rows // 8, screen_step, 0)
        if whole8 < rows:
            value = basis[whole8:rows, 0:LANES] * wide[0][0 : rows - whole8]
            for q in range(1, kk // LANES):
                value = value + (
                    basis[whole8:rows, q * LANES : (q + 1) * LANES] * wide[q][0 : rows - whole8]
                )
            target[whole8:rows, :] = value
        screen = jnp.sum(target[...], axis=1, keepdims=True)
        hot = ones3[:, 0:sp].astype(jnp.float32)
        for part, piece in enumerate(split3(screen)):
            place[:, part * sp : (part + 1) * sp] = (
                hot * piece.astype(jnp.float32)
            ).astype(jnp.bfloat16)
        placed = dot32(place[...], oned[...], 0, 0)
        split_out(placed[0:sp] + placed[sp : 2 * sp] + placed[2 * sp : 3 * sp])
        ebuf[me] = stage[me]
        scatter_start(4, ebuf)
        finish(4, ebuf)
        fbuf[me] = total(ebuf)
        gather_start(3, fbuf)
        finish(3, fbuf)
        return carry

    lax.fori_loop(0, ITERS, iteration, 0)
    join(fbuf, tec)
    tec_out[0] = tec[0 : tec0_ref.shape[1], 0:srcs]


def per_device(
    n, slots,
    measured_real, measured_imaginary, measured_weight, baseline_vectors, antenna_pairs,
    directions, direction_flux, channel_frequency, electron_content_start,
    pierce_station_direction, eigen_basis, eigen_weight,
):
    shard_slots, shard_channels, base_n = measured_real.shape
    assert shard_slots == 1 and shard_channels == 1
    stations, srcs = electron_content_start.shape[1:]
    rows, kk = eigen_basis.shape
    tiles = -(-base_n // TILE)
    drows = round_up(srcs, 16)
    dp = round_up(srcs, LANES)
    sp = round_up(stations, 64)
    cr = sp * (dp // LANES) // n
    rpad = round_up(rows + 1, 16)
    cw = kk // n
    assert cr * n == sp * (dp // LANES) and cw * n == kk and kk % LANES == 0
    groups = 1 + len({1 % slots, (slots - 1) % slots} - {0})

    own = lax.dynamic_slice_in_dim(
        pierce_station_direction[0], lax.axis_index("chan") * rows, rows, 0
    )
    own = jnp.pad(own, (0, rpad - rows), constant_values=-1)[:, None]
    smap = jnp.where(own < 0, -1, own // srcs)
    dmap = jnp.where(own < 0, -1, own % srcs)
    pairs = jnp.pad(antenna_pairs, ((0, 0), (0, tiles * TILE - base_n)), constant_values=-1)
    cols = jnp.pad(
        jnp.concatenate([direction_flux, directions], axis=0).T, ((0, drows - srcs), (0, 0))
    )
    f32, bf16 = jnp.float32, jnp.bfloat16
    vmem = pl.BlockSpec(memory_space=pltpu.VMEM)
    geo = (n, slots, tiles, base_n, srcs, drows, sp, dp, cr, rows, rpad, kk, cw)
    tec_final, coefficients, res_re, res_im = pl.pallas_call(
        functools.partial(solve_kernel, geo),
        out_shape=(
            jax.ShapeDtypeStruct((1, stations, srcs), f32),
            jax.ShapeDtypeStruct((1, kk), f32),
            jax.ShapeDtypeStruct((tiles, 1, TILE), f32),
            jax.ShapeDtypeStruct((tiles, 1, TILE), f32),
        ),
        in_specs=[vmem] * 11 + [pl.BlockSpec(memory_space=pl.ANY)] + [vmem],
        out_specs=(vmem,) * 4,
        scratch_shapes=[
            pltpu.VMEM((tiles, 1, TILE), f32),
            pltpu.VMEM((tiles, 1, TILE), f32),
            pltpu.VMEM((tiles, 1, TILE), f32),
            pltpu.VMEM((tiles, drows, TILE), f32),
            pltpu.VMEM((tiles, 3 * sp, TILE), bf16),
            pltpu.VMEM((tiles, sp, TILE), bf16),
            pltpu.VMEM((drows, TILE), f32),
            pltpu.VMEM((drows, TILE), f32),
            pltpu.VMEM((drows, TILE), f32),
            pltpu.VMEM((drows, TILE), f32),
            pltpu.VMEM((drows, TILE), bf16),
            pltpu.VMEM((drows, TILE), bf16),
            pltpu.VMEM((sp, dp), f32),
            pltpu.VMEM((dp, 3 * sp), bf16),
            pltpu.VMEM((sp, dp), f32),
            pltpu.VMEM((cr, LANES), f32),
            pltpu.VMEM((rows, kk), f32),
            pltpu.VMEM((rpad, 3 * sp), bf16),
            pltpu.VMEM((rpad, dp), bf16),
            pltpu.VMEM((rpad, dp), f32),
            pltpu.VMEM((rpad, LANES), f32),
            pltpu.VMEM((rpad, 3 * sp), bf16),
            pltpu.VMEM((n, cr, LANES), f32),
            pltpu.VMEM((n, cr, LANES), f32),
            pltpu.VMEM((n, cr, LANES), f32),
            pltpu.VMEM((n, 1, cw), f32),
            pltpu.VMEM((2, groups, n, 1, cw), f32),
            pltpu.VMEM((n, 1, cw), f32),
            pltpu.VMEM((n, cr, LANES), f32),
            pltpu.VMEM((n, cr, LANES), f32),
            pltpu.SemaphoreType.DMA,
            pltpu.SemaphoreType.DMA((5, n)),
            pltpu.SemaphoreType.DMA((5, n)),
            pltpu.SemaphoreType.DMA((groups, n)),
            pltpu.SemaphoreType.DMA((2, groups, n)),
        ],
        compiler_params=pltpu.CompilerParams(
            collective_id=0, has_side_effects=True, vmem_limit_bytes=60 * 1024 * 1024
        ),
    )(
        measured_real, measured_imaginary, measured_weight, baseline_vectors, pairs, cols,
        direction_flux, channel_frequency.reshape(1, 1), electron_content_start,
        smap, dmap, eigen_basis, eigen_weight.reshape(1, kk),
    )
    res_re = res_re.reshape(1, 1, tiles * TILE)[:, :, :base_n]
    res_im = res_im.reshape(1, 1, tiles * TILE)[:, :, :base_n]
    return tec_final, coefficients, res_re, res_im


def solution(mesh):
    in_specs = (
        P("slot", "chan", None),
        P("slot", "chan", None),
        P("slot", "chan", None),
        P("slot", None, None),
        P(),
        P(),
        P("chan", None),
        P("chan"),
        P("slot", None, None),
        P("slot", None),
        P("chan", None),
        P(),
    )
    out_specs = (
        P("slot", None, None),
        P("slot", None),
        P("slot", "chan", None),
        P("slot", "chan", None),
    )
    body = functools.partial(per_device, mesh.shape["chan"], mesh.shape["slot"])
    return jax.shard_map(body, mesh=mesh, in_specs=in_specs, out_specs=out_specs, check_vma=False)
```

```python
import functools

import jax
import jax.numpy as jnp
from jax import lax
from jax.experimental import pallas as pl
from jax.experimental.pallas import tpu as pltpu
from jax.sharding import PartitionSpec as P

ITERS = 4
TEC_PHASE = -0.8448
SMOOTHING = 0.5
TWO_PI = 6.283185307179586
LANES = 128
TILE = 256

COS_TERMS = ()
SIN_TERMS = ()


def _fit():
    import numpy as np

    nodes = 4000
    theta = np.pi * (np.arange(nodes) + 0.5) / nodes
    u = 0.125 * (1.0 + np.cos(theta))
    r = np.sqrt(u)
    out = []
    for values in (np.cos(2 * np.pi * r), np.sin(2 * np.pi * r) / r):
        cheb = np.polynomial.chebyshev.Chebyshev.fit(u, values, 7, domain=[0.0, 0.25])
        coefs = cheb.convert(kind=np.polynomial.Polynomial).coef
        out.append(tuple(float(np.float32(c)) for c in coefs))
    return out


COS_TERMS, SIN_TERMS = _fit()


def round_up(value, unit):
    return -(-value // unit) * unit


def horner(terms, u):
    acc = jnp.full_like(u, terms[-1])
    for term in terms[-2::-1]:
        acc = acc * u + term
    return acc


def split3(x):
    hi = x.astype(jnp.bfloat16)
    rest = x - hi.astype(jnp.float32)
    mid = rest.astype(jnp.bfloat16)
    low = (rest - mid.astype(jnp.float32)).astype(jnp.bfloat16)
    return hi, mid, low


def dot32(a, b, ca, cb):
    return lax.dot_general(a, b, (((ca,), (cb,)), ((), ())), preferred_element_type=jnp.float32)


def solve_kernel(
    geo,
    vr_ref, vi_ref, w_ref, bv_ref, pairs_ref, dir_ref, flux_ref, freq_ref, tec0_ref,
    own_ref, basis_ref, ew_ref,
    tec_out, coef_out, rr_out, ri_out,
    resr, resi, cols, mapt, visr, visi, wt, geom, sign3, sgn, fluxb, phase, mre, mim, phi, plo,
    tec, tec3, acc, den, basis, ones3, oned, onedf, target, place,
    stage, abuf, bbuf, craw, cbuf, dbuf, ebuf, fbuf,
    basis_sem, send_sem, recv_sem, csend, crecv,
):
    n, slots, tiles, base_n, srcs, drows, sp, dp, cr, rows, rpad, kk, cw = geo
    me = lax.axis_index("chan")
    slot = lax.axis_index("slot")
    offs = sorted({1 % slots, (slots - 1) % slots} - {0})

    def peer(k):
        return lax.rem(me + k, n)

    bits = n.bit_length() - 1
    if n == 1 << bits:
        flips = []
        rest = me
        for b in range(bits):
            flips.append((1 - 2 * lax.rem(rest, 2)) * (1 << b))
            rest = rest // 2

        def partner(k):
            to = me
            for b in range(bits):
                if (k >> b) & 1:
                    to = to + flips[b]
            return to
    else:
        partner = peer

    whole8 = rows // 8 * 8
    load = pltpu.make_async_copy(basis_ref, basis, basis_sem)
    load.start()

    barrier = pltpu.get_barrier_semaphore()

    def greet(k, c):
        pl.semaphore_signal(
            barrier, inc=1, device_id={"chan": peer(k), "slot": slot},
            device_id_type=pl.DeviceIdType.MESH,
        )
        return c

    lax.fori_loop(1, n, greet, 0)
    for off in offs:

        def greet_far(k, c, off=off):
            pl.semaphore_signal(
                barrier, inc=1,
                device_id={"chan": peer(k), "slot": lax.rem(slot + off, slots)},
                device_id_type=pl.DeviceIdType.MESH,
            )
            return c

        lax.fori_loop(0, n, greet_far, 0)

    freq = jnp.full((1, 1), freq_ref[0], jnp.float32)
    scale = TEC_PHASE / freq
    turn_scale = (TEC_PHASE / TWO_PI) / freq
    acc[...] = jnp.zeros((sp, dp), jnp.float32)
    acc[0:1, 0:srcs] = flux_ref[...]
    acc[1:4, 0:srcs] = dir_ref[...]
    flux_row = acc[0:1, :]
    cols[...] = acc[0:8, :].T
    fluxb[...] = jnp.broadcast_to(cols[0:drows, 0:1], (drows, TILE))
    weight_sum = jnp.zeros((sp, 1), jnp.float32)
    for j in range(tiles):
        lo = j * TILE
        width = min(TILE, base_n - lo)
        if width < TILE:
            sgn[j] = jnp.zeros((sp, TILE), jnp.bfloat16)
            sign3[j] = jnp.zeros((3 * sp, TILE), jnp.bfloat16)
            geom[j] = jnp.zeros((drows, TILE), jnp.float32)
        for dst, src in ((visr, vr_ref), (visi, vi_ref), (wt, w_ref)):
            if width < TILE:
                dst[j] = jnp.zeros((1, TILE), jnp.float32)
            dst[j, :, 0:width] = src[0, :, lo : lo + width]
        station = lax.broadcasted_iota(jnp.int32, (sp, width), 0)
        first = (pairs_ref[0:1, lo : lo + width] == station).astype(jnp.float32)
        second = (pairs_ref[1:2, lo : lo + width] == station).astype(jnp.float32)
        weight_sum = weight_sum + jnp.sum(
            (first + second) * w_ref[0, :, lo : lo + width], axis=1, keepdims=True
        )
        packed = (first - second).astype(jnp.bfloat16)
        sgn[j, :, 0:width] = packed
        for part in range(3):
            sign3[j, part * sp : (part + 1) * sp, 0:width] = packed
        geom[j, :, 0:width] = (
            cols[0:drows, 1:2] * bv_ref[0, :, lo : lo + width]
            + cols[0:drows, 2:3] * bv_ref[1, :, lo : lo + width]
            + cols[0:drows, 3:4] * bv_ref[2, :, lo : lo + width]
        ) * freq

    def split_out(value):
        for j in range(n):
            top, left = (j // (dp // LANES)) * cr, (j % (dp // LANES)) * LANES
            stage[j] = value[top : top + cr, left : left + LANES]

    def copy_of(phase_id, src, dst, k, slot_of_src):
        to = partner(k)
        return pltpu.make_async_remote_copy(
            src_ref=src.at[to if slot_of_src else me], dst_ref=dst.at[me],
            send_sem=send_sem.at[phase_id, k], recv_sem=recv_sem.at[phase_id, me],
            device_id={"chan": to, "slot": slot}, device_id_type=pl.DeviceIdType.MESH,
        )

    def scatter_start(phase_id, dst):
        for k in range(n - 1, 0, -1):
            copy_of(phase_id, stage, dst, k, True).start()

    def gather_start(phase_id, dst):
        for k in range(n - 1, 0, -1):
            copy_of(phase_id, dst, dst, k, False).start()

    def receive(phase_id, dst):
        def one(k, c):
            src = peer(k)
            pltpu.make_async_remote_copy(
                src_ref=dst.at[src], dst_ref=dst.at[src],
                send_sem=send_sem.at[phase_id, 0], recv_sem=recv_sem.at[phase_id, src],
                device_id={"chan": src, "slot": slot}, device_id_type=pl.DeviceIdType.MESH,
            ).wait_recv()
            return c

        lax.fori_loop(1, n, one, 0)

    def drain(phase_id, dst):
        def one(k, c):
            pltpu.make_async_remote_copy(
                src_ref=dst.at[me], dst_ref=dst.at[me],
                send_sem=send_sem.at[phase_id, k], recv_sem=recv_sem.at[phase_id, me],
                device_id={"chan": peer(k), "slot": slot},
                device_id_type=pl.DeviceIdType.MESH,
            ).wait_send()
            return c

        lax.fori_loop(1, n, one, 0)

    def total(buf):
        value = buf[0]
        for j in range(1, n):
            value = value + buf[j]
        return value

    def join(buf, out):
        for j in range(n):
            top, left = (j // (dp // LANES)) * cr, (j % (dp // LANES)) * LANES
            out[top : top + cr, left : left + LANES] = buf[j]

    tec[...] = jnp.zeros((sp, dp), jnp.float32)
    for st in range(tec0_ref.shape[0]):
        tec[st : st + 1, 0:srcs] = tec0_ref[st]
    part_den = (weight_sum * (scale * scale)) * (flux_row * flux_row)
    for j in range(n):
        top, left = (j // (dp // LANES)) * cr, (j % (dp // LANES)) * LANES
        fbuf[j] = tec[top : top + cr, left : left + LANES]
    split_out(part_den)
    ebuf[me] = stage[me]

    mapt[...] = jnp.full(mapt.shape, -1.0, jnp.float32)
    mapt[:, 0:rows] = jnp.broadcast_to(own_ref[...].astype(jnp.float32), (8, rows))
    place_col = mapt[...].T[0:rpad, 0:1]
    station_col = jnp.floor((place_col + 0.5) * (1.0 / srcs))
    direction_col = place_col - station_col * srcs
    lane_s = lax.broadcasted_iota(jnp.int32, (rpad, sp), 1).astype(jnp.float32)
    hot_s = (station_col == lane_s).astype(jnp.float32)
    for part in range(3):
        ones3[:, part * sp : (part + 1) * sp] = hot_s.astype(jnp.bfloat16)
    lane_d = lax.broadcasted_iota(jnp.int32, (rpad, dp), 1).astype(jnp.float32)
    hot_d = ((direction_col == lane_d) & (place_col >= 0.0)).astype(jnp.float32)
    onedf[...] = hot_d
    oned[...] = hot_d.astype(jnp.bfloat16)

    pl.semaphore_wait(barrier, (n - 1) + n * len(offs))
    scatter_start(4, ebuf)

    last = slots - 1
    neighbours = jnp.where(slot > 0, 1.0, 0.0) + jnp.where(slot < last, 1.0, 0.0)

    def iteration(it, carry):
        par = lax.rem(it, 2)
        join(fbuf, tec)
        turned = (tec[...] * turn_scale).T
        for part, piece in enumerate(split3(turned)):
            tec3[:, part * sp : (part + 1) * sp] = piece
        acc[...] = jnp.zeros((sp, dp), jnp.float32)

        def pair_tile(j, c):
            phase[...] = dot32(tec3[0:drows, :], sign3[j], 1, 0) + geom[j]
            sum_re = jnp.zeros((8, TILE), jnp.float32)
            sum_im = jnp.zeros((8, TILE), jnp.float32)
            for top in range(0, drows, 16):
                t = phase[top : top + 16, :]
                r = t - jnp.round(t)
                u = r * r
                flux = fluxb[top : top + 16, :]
                re = horner(COS_TERMS, u) * flux
                im = horner(SIN_TERMS, u) * (r * flux)
                mre[top : top + 16, :] = re
                mim[top : top + 16, :] = im
                sum_re = sum_re + re[0:8] + re[8:16]
                sum_im = sum_im + im[0:8] + im[8:16]
            left_re = visr[j] - jnp.sum(sum_re, axis=0, keepdims=True)
            left_im = visi[j] - jnp.sum(sum_im, axis=0, keepdims=True)
            resr[j] = left_re
            resi[j] = left_im
            wre = wt[j] * left_re
            wim = wt[j] * left_im
            for top in range(0, drows, 16):
                p = mre[top : top + 16, :] * wim - mim[top : top + 16, :] * wre
                hi = p.astype(jnp.bfloat16)
                phi[top : top + 16, :] = hi
                plo[top : top + 16, :] = (p - hi.astype(jnp.float32)).astype(jnp.bfloat16)
            acc[:, 0:drows] += dot32(sgn[j], phi[...], 1, 1) + dot32(sgn[j], plo[...], 1, 1)
            return c

        lax.fori_loop(0, tiles, pair_tile, 0)

        @pl.when(it == 0)
        def _():
            drain(4, ebuf)

        @pl.when(it > 0)
        def _():
            drain(3, fbuf)

        split_out(acc[...] * scale)
        scatter_start(0, abuf)
        abuf[me] = stage[me]

        @pl.when(it == 0)
        def _():
            receive(4, ebuf)
            den_sum = total(ebuf)
            den[...] = jnp.where(den_sum == 0.0, 1.0, den_sum)
            load.wait()

        receive(0, abuf)
        bbuf[me] = fbuf[me] + total(abuf) / den[...]
        gather_start(1, bbuf)
        drain(0, abuf)
        receive(1, bbuf)
        join(bbuf, acc)

        field = jnp.concatenate([x for x in split3(acc[...])], axis=0)
        picked = dot32(ones3[...], field, 1, 0) * onedf[...]
        target[...] = jnp.broadcast_to(jnp.sum(picked, axis=1, keepdims=True), (rpad, LANES))

        def raw_step(i, sums):
            at = pl.ds(pl.multiple_of(i * 8, 8), 8)
            t = target[at, :]
            return tuple(
                s + basis[at, q * LANES : (q + 1) * LANES] * t for q, s in enumerate(sums)
            )

        zero = jnp.zeros((8, LANES), jnp.float32)
        sums = lax.fori_loop(0, rows // 8, raw_step, tuple(zero for _ in range(kk // LANES)))
        row = jnp.concatenate([jnp.sum(s, axis=0, keepdims=True) for s in sums], axis=1)
        if whole8 < rows:
            rest = target[whole8:rows, 0:1] * basis[whole8:rows, :]
            row = row + jnp.sum(rest, axis=0, keepdims=True)
        row = row * ew_ref[...]
        for j in range(n):
            craw[j] = row[:, j * cw : (j + 1) * cw]
        cbuf[par, 0, me] = craw[me]

        def c_copy(g, off, to, src, k):
            return pltpu.make_async_remote_copy(
                src_ref=craw.at[to], dst_ref=cbuf.at[par, g, src],
                send_sem=csend.at[g, k], recv_sem=crecv.at[par, g, src],
                device_id={"chan": to, "slot": lax.rem(slot + off, slots)},
                device_id_type=pl.DeviceIdType.MESH,
            )

        groups = [0] + offs
        for k in range(n - 1, -1, -1):
            for g, off in reversed(list(enumerate(groups))):
                if k or off:
                    c_copy(g, off, partner(k), me, k).start()
        drain(1, bbuf)
        for g, off in enumerate(groups):

            def wait_one(k, c, g=g, off=off):
                c_copy(g, off, peer(k), peer(k), k).wait_recv()
                return c

            lax.fori_loop(1 if off == 0 else 0, n, wait_one, 0)
        smooth = total(cbuf.at[par, 0])
        for g, off in enumerate(groups):
            if off:
                source = lax.rem(slot - off + slots, slots)
                near = jnp.abs(source - slot) == 1
                smooth = smooth + total(cbuf.at[par, g]) * jnp.where(near, SMOOTHING, 0.0)
        dbuf[me] = smooth / (1.0 + SMOOTHING * neighbours)
        gather_start(2, dbuf)
        for g, off in enumerate(groups):

            def drain_one(k, c, g=g, off=off):
                c_copy(g, off, peer(k), peer(k), k).wait_send()
                return c

            lax.fori_loop(1 if off == 0 else 0, n, drain_one, 0)
        receive(2, dbuf)
        coef = jnp.concatenate([dbuf[j] for j in range(n)], axis=1)
        coef_out[...] = coef
        wide = [
            jnp.broadcast_to(coef[:, q * LANES : (q + 1) * LANES], (8, LANES))
            for q in range(kk // LANES)
        ]

        def screen_step(i, c):
            at = pl.ds(pl.multiple_of(i * 8, 8), 8)
            value = basis[at, 0:LANES] * wide[0]
            for q in range(1, kk // LANES):
                value = value + basis[at, q * LANES : (q + 1) * LANES] * wide[q]
            target[at, :] = value
            return c

        lax.fori_loop(0, rows // 8, screen_step, 0)
        if whole8 < rows:
            value = basis[whole8:rows, 0:LANES] * wide[0][0 : rows - whole8]
            for q in range(1, kk // LANES):
                value = value + (
                    basis[whole8:rows, q * LANES : (q + 1) * LANES] * wide[q][0 : rows - whole8]
                )
            target[whole8:rows, :] = value
        screen = jnp.sum(target[...], axis=1, keepdims=True)
        hot = ones3[:, 0:sp].astype(jnp.float32)
        for part, piece in enumerate(split3(screen)):
            place[:, part * sp : (part + 1) * sp] = (
                hot * piece.astype(jnp.float32)
            ).astype(jnp.bfloat16)
        placed = dot32(place[...], oned[...], 0, 0)
        split_out(placed[0:sp] + placed[sp : 2 * sp] + placed[2 * sp : 3 * sp])
        scatter_start(4, ebuf)
        ebuf[me] = stage[me]
        drain(2, dbuf)
        receive(4, ebuf)
        fbuf[me] = total(ebuf)
        gather_start(3, fbuf)
        drain(4, ebuf)
        receive(3, fbuf)
        return carry

    lax.fori_loop(0, ITERS, iteration, 0)
    drain(3, fbuf)
    join(fbuf, tec)
    for st in range(tec0_ref.shape[0]):
        tec_out[st] = tec[st : st + 1, 0:srcs]
    for j in range(tiles):
        lo = j * TILE
        width = min(TILE, base_n - lo)
        rr_out[0, :, lo : lo + width] = resr[j, :, 0:width]
        ri_out[0, :, lo : lo + width] = resi[j, :, 0:width]


def per_device(
    n, slots,
    measured_real, measured_imaginary, measured_weight, baseline_vectors, antenna_pairs,
    directions, direction_flux, channel_frequency, electron_content_start,
    pierce_station_direction, eigen_basis, eigen_weight,
):
    shard_slots, shard_channels, base_n = measured_real.shape
    assert shard_slots == 1 and shard_channels == 1
    stations, srcs = electron_content_start.shape[1:]
    rows, kk = eigen_basis.shape
    tiles = -(-base_n // TILE)
    drows = round_up(srcs, 16)
    dp = round_up(srcs, LANES)
    sp = round_up(stations, 64)
    cr = sp * (dp // LANES) // n
    rpad = round_up(rows + 1, 16)
    cw = kk // n
    assert cr * n == sp * (dp // LANES) and cw * n == kk and kk % LANES == 0
    groups = 1 + len({1 % slots, (slots - 1) % slots} - {0})

    own = lax.dynamic_slice_in_dim(
        pierce_station_direction[0], lax.axis_index("chan") * rows, rows, 0
    )
    f32, bf16 = jnp.float32, jnp.bfloat16
    vmem = pl.BlockSpec(memory_space=pltpu.VMEM)
    geo = (n, slots, tiles, base_n, srcs, drows, sp, dp, cr, rows, rpad, kk, cw)
    tec_final, coefficients, res_re, res_im = pl.pallas_call(
        functools.partial(solve_kernel, geo),
        out_shape=(
            jax.ShapeDtypeStruct((stations, 1, srcs), f32),
            jax.ShapeDtypeStruct((1, kk), f32),
            jax.ShapeDtypeStruct((1, 1, base_n), f32),
            jax.ShapeDtypeStruct((1, 1, base_n), f32),
        ),
        in_specs=[vmem] * 7
        + [pl.BlockSpec(memory_space=pltpu.SMEM)]
        + [vmem] * 2
        + [pl.BlockSpec(memory_space=pl.ANY)]
        + [vmem],
        out_specs=(vmem,) * 4,
        scratch_shapes=[
            pltpu.VMEM((tiles, 1, TILE), f32),
            pltpu.VMEM((tiles, 1, TILE), f32),
            pltpu.VMEM((dp, 8), f32),
            pltpu.VMEM((8, round_up(rpad, LANES)), f32),
            pltpu.VMEM((tiles, 1, TILE), f32),
            pltpu.VMEM((tiles, 1, TILE), f32),
            pltpu.VMEM((tiles, 1, TILE), f32),
            pltpu.VMEM((tiles, drows, TILE), f32),
            pltpu.VMEM((tiles, 3 * sp, TILE), bf16),
            pltpu.VMEM((tiles, sp, TILE), bf16),
            pltpu.VMEM((drows, TILE), f32),
            pltpu.VMEM((drows, TILE), f32),
            pltpu.VMEM((drows, TILE), f32),
            pltpu.VMEM((drows, TILE), f32),
            pltpu.VMEM((drows, TILE), bf16),
            pltpu.VMEM((drows, TILE), bf16),
            pltpu.VMEM((sp, dp), f32),
            pltpu.VMEM((dp, 3 * sp), bf16),
            pltpu.VMEM((sp, dp), f32),
            pltpu.VMEM((cr, LANES), f32),
            pltpu.VMEM((rows, kk), f32),
            pltpu.VMEM((rpad, 3 * sp), bf16),
            pltpu.VMEM((rpad, dp), bf16),
            pltpu.VMEM((rpad, dp), f32),
            pltpu.VMEM((rpad, LANES), f32),
            pltpu.VMEM((rpad, 3 * sp), bf16),
            pltpu.VMEM((n, cr, LANES), f32),
            pltpu.VMEM((n, cr, LANES), f32),
            pltpu.VMEM((n, cr, LANES), f32),
            pltpu.VMEM((n, 1, cw), f32),
            pltpu.VMEM((2, groups, n, 1, cw), f32),
            pltpu.VMEM((n, 1, cw), f32),
            pltpu.VMEM((n, cr, LANES), f32),
            pltpu.VMEM((n, cr, LANES), f32),
            pltpu.SemaphoreType.DMA,
            pltpu.SemaphoreType.DMA((5, n)),
            pltpu.SemaphoreType.DMA((5, n)),
            pltpu.SemaphoreType.DMA((groups, n)),
            pltpu.SemaphoreType.DMA((2, groups, n)),
        ],
        compiler_params=pltpu.CompilerParams(
            collective_id=0, has_side_effects=True, vmem_limit_bytes=60 * 1024 * 1024
        ),
    )(
        measured_real, measured_imaginary, measured_weight,
        baseline_vectors.reshape(3, 1, base_n), antenna_pairs, directions,
        direction_flux, channel_frequency, electron_content_start.reshape(stations, 1, srcs),
        own.reshape(1, rows), eigen_basis, eigen_weight.reshape(1, kk),
    )
    return tec_final.reshape(1, stations, srcs), coefficients, res_re, res_im


def solution(mesh):
    in_specs = (
        P("slot", "chan", None),
        P("slot", "chan", None),
        P("slot", "chan", None),
        P("slot", None, None),
        P(),
        P(),
        P("chan", None),
        P("chan"),
        P("slot", None, None),
        P("slot", None),
        P("chan", None),
        P(),
    )
    out_specs = (
        P("slot", None, None),
        P("slot", None),
        P("slot", "chan", None),
        P("slot", "chan", None),
    )
    body = functools.partial(per_device, mesh.shape["chan"], mesh.shape["slot"])
    return jax.shard_map(body, mesh=mesh, in_specs=in_specs, out_specs=out_specs, check_vma=False)
```

```python
import functools

import jax
import jax.numpy as jnp
from jax import lax
from jax.experimental import pallas as pl
from jax.experimental.pallas import tpu as pltpu
from jax.sharding import PartitionSpec as P

ITERS = 4
TEC_PHASE = -0.8448
SMOOTHING = 0.5
TWO_PI = 6.283185307179586
LANES = 128
TILE = 256

COS_TERMS = ()
SIN_TERMS = ()


def _fit():
    import numpy as np

    nodes = 4000
    theta = np.pi * (np.arange(nodes) + 0.5) / nodes
    u = 0.125 * (1.0 + np.cos(theta))
    r = np.sqrt(u)
    out = []
    for values in (np.cos(2 * np.pi * r), np.sin(2 * np.pi * r) / r):
        cheb = np.polynomial.chebyshev.Chebyshev.fit(u, values, 6, domain=[0.0, 0.25])
        coefs = cheb.convert(kind=np.polynomial.Polynomial).coef
        out.append(tuple(float(np.float32(c)) for c in coefs))
    return out


COS_TERMS, SIN_TERMS = _fit()


def round_up(value, unit):
    return -(-value // unit) * unit


def horner(terms, u):
    acc = jnp.full_like(u, terms[-1])
    for term in terms[-2::-1]:
        acc = acc * u + term
    return acc


def split3(x):
    hi = x.astype(jnp.bfloat16)
    rest = x - hi.astype(jnp.float32)
    mid = rest.astype(jnp.bfloat16)
    low = (rest - mid.astype(jnp.float32)).astype(jnp.bfloat16)
    return hi, mid, low


def dot32(a, b, ca, cb):
    return lax.dot_general(a, b, (((ca,), (cb,)), ((), ())), preferred_element_type=jnp.float32)


def solve_kernel(
    geo,
    vr_ref, vi_ref, w_ref, bv_ref, pairs_ref, dir_ref, flux_ref, freq_ref, tec0_ref,
    own_ref, basis_ref, ew_ref,
    tec_out, coef_out, rr_out, ri_out,
    resr, resi, cols, mapt, visr, visi, wt, geom, sign3, sgn, fluxb, phase, mre, mim, phi, plo,
    tec, tec3, acc, den, basis, ones3, oned, onedf, target, place,
    stage, abuf, bbuf, craw, cbuf, dbuf, ebuf, fbuf,
    psum_in, basis_sem, send_sem, recv_sem, csend, crecv, swap_send, swap_recv,
):
    n, slots, tiles, base_n, srcs, drows, sp, dp, cr, rows, rpad, kk = geo
    me = lax.axis_index("chan")
    slot = lax.axis_index("slot")
    offs = sorted({1 % slots, (slots - 1) % slots} - {0})

    def peer(k):
        return lax.rem(me + k, n)

    bits = n.bit_length() - 1
    if n == 1 << bits:
        flips = []
        rest = me
        for b in range(bits):
            flips.append((1 - 2 * lax.rem(rest, 2)) * (1 << b))
            rest = rest // 2

        def partner(k):
            to = me
            for b in range(bits):
                if (k >> b) & 1:
                    to = to + flips[b]
            return to
    else:
        partner = peer

    whole8 = rows // 8 * 8
    burst = max(f for f in (1, 2, 3) if (rows // 8) % f == 0)
    load = pltpu.make_async_copy(basis_ref, basis, basis_sem)
    load.start()

    barrier = pltpu.get_barrier_semaphore()

    def greet(k, c):
        pl.semaphore_signal(
            barrier, inc=1, device_id={"chan": peer(k), "slot": slot},
            device_id_type=pl.DeviceIdType.MESH,
        )
        return c

    lax.fori_loop(1, n, greet, 0)
    for off in offs:

        def greet_far(k, c, off=off):
            pl.semaphore_signal(
                barrier, inc=1,
                device_id={"chan": peer(k), "slot": lax.rem(slot + off, slots)},
                device_id_type=pl.DeviceIdType.MESH,
            )
            return c

        lax.fori_loop(0, n, greet_far, 0)

    freq = jnp.full((1, 1), freq_ref[0], jnp.float32)
    scale = TEC_PHASE / freq
    turn_scale = (TEC_PHASE / TWO_PI) / freq
    acc[...] = jnp.zeros((sp, dp), jnp.float32)
    acc[0:1, 0:srcs] = flux_ref[...]
    acc[1:4, 0:srcs] = dir_ref[...]
    flux_row = acc[0:1, :]
    cols[...] = acc[0:8, :].T
    fluxb[...] = jnp.broadcast_to(cols[0:drows, 0:1], (drows, TILE))
    weight_sum = jnp.zeros((sp, 1), jnp.float32)
    for j in range(tiles):
        lo = j * TILE
        width = min(TILE, base_n - lo)
        if width < TILE:
            sgn[j] = jnp.zeros((sp, TILE), jnp.bfloat16)
            sign3[j] = jnp.zeros((3 * sp, TILE), jnp.bfloat16)
            geom[j] = jnp.zeros((drows, TILE), jnp.float32)
        for dst, src in ((visr, vr_ref), (visi, vi_ref), (wt, w_ref)):
            if width < TILE:
                dst[j] = jnp.zeros((1, TILE), jnp.float32)
            dst[j, :, 0:width] = src[0, :, lo : lo + width]
        station = lax.broadcasted_iota(jnp.int32, (sp, width), 0)
        first = (pairs_ref[0:1, lo : lo + width] == station).astype(jnp.float32)
        second = (pairs_ref[1:2, lo : lo + width] == station).astype(jnp.float32)
        weight_sum = weight_sum + jnp.sum(
            (first + second) * w_ref[0, :, lo : lo + width], axis=1, keepdims=True
        )
        packed = (first - second).astype(jnp.bfloat16)
        sgn[j, :, 0:width] = packed
        for part in range(3):
            sign3[j, part * sp : (part + 1) * sp, 0:width] = packed
        geom[j, :, 0:width] = (
            cols[0:drows, 1:2] * bv_ref[0, :, lo : lo + width]
            + cols[0:drows, 2:3] * bv_ref[1, :, lo : lo + width]
            + cols[0:drows, 3:4] * bv_ref[2, :, lo : lo + width]
        ) * freq

    def split_out(value):
        for j in range(n):
            top, left = (j // (dp // LANES)) * cr, (j % (dp // LANES)) * LANES
            stage[j] = value[top : top + cr, left : left + LANES]

    def copy_of(phase_id, src, dst, k, slot_of_src):
        to = partner(k)
        return pltpu.make_async_remote_copy(
            src_ref=src.at[to if slot_of_src else me], dst_ref=dst.at[me],
            send_sem=send_sem.at[phase_id, k], recv_sem=recv_sem.at[phase_id, me],
            device_id={"chan": to, "slot": slot}, device_id_type=pl.DeviceIdType.MESH,
        )

    def scatter_start(phase_id, dst):
        for k in range(n - 1, 0, -1):
            copy_of(phase_id, stage, dst, k, True).start()

    def gather_start(phase_id, dst):
        for k in range(n - 1, 0, -1):
            copy_of(phase_id, dst, dst, k, False).start()

    def receive(phase_id, dst):
        def one(k, c):
            src = peer(k)
            pltpu.make_async_remote_copy(
                src_ref=dst.at[src], dst_ref=dst.at[src],
                send_sem=send_sem.at[phase_id, 0], recv_sem=recv_sem.at[phase_id, src],
                device_id={"chan": src, "slot": slot}, device_id_type=pl.DeviceIdType.MESH,
            ).wait_recv()
            return c

        lax.fori_loop(1, n, one, 0)

    def drain(phase_id, dst):
        def one(k, c):
            pltpu.make_async_remote_copy(
                src_ref=dst.at[me], dst_ref=dst.at[me],
                send_sem=send_sem.at[phase_id, k], recv_sem=recv_sem.at[phase_id, me],
                device_id={"chan": peer(k), "slot": slot},
                device_id_type=pl.DeviceIdType.MESH,
            ).wait_send()
            return c

        lax.fori_loop(1, n, one, 0)

    def total(buf):
        value = buf[0]
        for j in range(1, n):
            value = value + buf[j]
        return value

    def join(buf, out):
        for j in range(n):
            top, left = (j // (dp // LANES)) * cr, (j % (dp // LANES)) * LANES
            out[top : top + cr, left : left + LANES] = buf[j]

    tec[...] = jnp.zeros((sp, dp), jnp.float32)
    for st in range(tec0_ref.shape[0]):
        tec[st : st + 1, 0:srcs] = tec0_ref[st]
    part_den = (weight_sum * (scale * scale)) * (flux_row * flux_row)
    for j in range(n):
        top, left = (j // (dp // LANES)) * cr, (j % (dp // LANES)) * LANES
        fbuf[j] = tec[top : top + cr, left : left + LANES]
    split_out(part_den)
    ebuf[me] = stage[me]

    mapt[...] = jnp.full(mapt.shape, -1.0, jnp.float32)
    mapt[:, 0:rows] = jnp.broadcast_to(own_ref[...].astype(jnp.float32), (8, rows))
    place_col = mapt[...].T[0:rpad, 0:1]
    station_col = jnp.floor((place_col + 0.5) * (1.0 / srcs))
    direction_col = place_col - station_col * srcs
    lane_s = lax.broadcasted_iota(jnp.int32, (rpad, sp), 1).astype(jnp.float32)
    hot_s = (station_col == lane_s).astype(jnp.float32)
    for part in range(3):
        ones3[:, part * sp : (part + 1) * sp] = hot_s.astype(jnp.bfloat16)
    lane_d = lax.broadcasted_iota(jnp.int32, (rpad, dp), 1).astype(jnp.float32)
    hot_d = ((direction_col == lane_d) & (place_col >= 0.0)).astype(jnp.float32)
    onedf[...] = hot_d
    oned[...] = hot_d.astype(jnp.bfloat16)

    pl.semaphore_wait(barrier, (n - 1) + n * len(offs))
    scatter_start(4, ebuf)

    core = lax.rem(me, 2)
    chip = me // 2
    chips, half = n // 2, kk // 2

    def swap(which, src, dst):
        return pltpu.make_async_remote_copy(
            src_ref=src, dst_ref=dst,
            send_sem=swap_send.at[which], recv_sem=swap_recv.at[which],
            device_id={"chan": me + 1 - 2 * core, "slot": slot},
            device_id_type=pl.DeviceIdType.MESH,
        )

    last = slots - 1
    neighbours = jnp.where(slot > 0, 1.0, 0.0) + jnp.where(slot < last, 1.0, 0.0)

    def iteration(it, carry):
        par = lax.rem(it, 2)
        join(fbuf, tec)
        turned = (tec[...] * turn_scale).T
        for part, piece in enumerate(split3(turned)):
            tec3[:, part * sp : (part + 1) * sp] = piece
        acc[...] = jnp.zeros((sp, dp), jnp.float32)

        def pair_tile(j, c):
            phase[...] = dot32(tec3[0:drows, :], sign3[j], 1, 0) + geom[j]
            sum_re = jnp.zeros((8, TILE), jnp.float32)
            sum_im = jnp.zeros((8, TILE), jnp.float32)
            for top in range(0, drows, 16):
                t = phase[top : top + 16, :]
                r = t - jnp.round(t)
                u = r * r
                flux = fluxb[top : top + 16, :]
                re = horner(COS_TERMS, u) * flux
                im = horner(SIN_TERMS, u) * (r * flux)
                mre[top : top + 16, :] = re
                mim[top : top + 16, :] = im
                sum_re = sum_re + re[0:8] + re[8:16]
                sum_im = sum_im + im[0:8] + im[8:16]
            left_re = visr[j] - jnp.sum(sum_re, axis=0, keepdims=True)
            left_im = visi[j] - jnp.sum(sum_im, axis=0, keepdims=True)
            resr[j] = left_re
            resi[j] = left_im
            wre = wt[j] * left_re
            wim = wt[j] * left_im
            for top in range(0, drows, 16):
                p = mre[top : top + 16, :] * wim - mim[top : top + 16, :] * wre
                hi = p.astype(jnp.bfloat16)
                phi[top : top + 16, :] = hi
                plo[top : top + 16, :] = (p - hi.astype(jnp.float32)).astype(jnp.bfloat16)
            acc[:, 0:drows] += dot32(sgn[j], phi[...], 1, 1) + dot32(sgn[j], plo[...], 1, 1)
            return c

        lax.fori_loop(0, tiles, pair_tile, 0)

        @pl.when(it == 0)
        def _():
            drain(4, ebuf)

        @pl.when(it > 0)
        def _():
            drain(3, fbuf)

        split_out(acc[...] * scale)
        scatter_start(0, abuf)
        abuf[me] = stage[me]

        @pl.when(it == 0)
        def _():
            receive(4, ebuf)
            den_sum = total(ebuf)
            den[...] = jnp.where(den_sum == 0.0, 1.0, den_sum)
            load.wait()

        receive(0, abuf)
        bbuf[me] = fbuf[me] + total(abuf) / den[...]
        gather_start(1, bbuf)
        drain(0, abuf)
        receive(1, bbuf)
        join(bbuf, acc)

        field = jnp.concatenate([x for x in split3(acc[...])], axis=0)
        picked = dot32(ones3[...], field, 1, 0) * onedf[...]
        target[...] = jnp.broadcast_to(jnp.sum(picked, axis=1, keepdims=True), (rpad, LANES))

        def raw_step(i, sums):
            for part in range(burst):
                at = pl.ds(pl.multiple_of((i * burst + part) * 8, 8), 8)
                t = target[at, :]
                sums = tuple(
                    s + basis[at, q * LANES : (q + 1) * LANES] * t for q, s in enumerate(sums)
                )
            return sums

        zero = jnp.zeros((8, LANES), jnp.float32)
        sums = lax.fori_loop(0, rows // 8 // burst, raw_step, tuple(zero for _ in range(kk // LANES)))
        row = jnp.concatenate([jnp.sum(s, axis=0, keepdims=True) for s in sums], axis=1)
        if whole8 < rows:
            rest = target[whole8:rows, 0:1] * basis[whole8:rows, :]
            row = row + jnp.sum(rest, axis=0, keepdims=True)
        row = row * ew_ref[...]
        for h in range(2):
            for q in range(half // LANES):
                lo = h * half + q * LANES
                craw[h, q : q + 1, :] = row[:, lo : lo + LANES]
        swap(0, craw.at[1 - core], psum_in.at[0]).start()
        drain(1, bbuf)
        swap(0, craw.at[1 - core], psum_in.at[0]).wait()
        mine = craw[core] + psum_in[0]
        cbuf[par, 0, chip] = mine

        def c_copy(g, off, to, src, k):
            return pltpu.make_async_remote_copy(
                src_ref=cbuf.at[par, 0, chip], dst_ref=cbuf.at[par, g, src],
                send_sem=csend.at[g, k], recv_sem=crecv.at[par, g, src],
                device_id={"chan": 2 * to + core, "slot": lax.rem(slot + off, slots)},
                device_id_type=pl.DeviceIdType.MESH,
            )

        groups = [0] + offs
        for k in range(chips - 1, -1, -1):
            for g, off in reversed(list(enumerate(groups))):
                if k or off:
                    c_copy(g, off, partner(2 * k) // 2, chip, k).start()
        for g, off in enumerate(groups):
            for k in range(0 if off else 1, chips):
                src = lax.rem(chip + k, chips)
                c_copy(g, off, src, src, k).wait_recv()

        def chip_total(g):
            value = cbuf[par, g, 0]
            for j in range(1, chips):
                value = value + cbuf[par, g, j]
            return value

        smooth = chip_total(0)
        for g, off in enumerate(groups):
            if off:
                source = lax.rem(slot - off + slots, slots)
                near = jnp.abs(source - slot) == 1
                smooth = smooth + chip_total(g) * jnp.where(near, SMOOTHING, 0.0)
        dbuf[core] = smooth / (1.0 + SMOOTHING * neighbours)
        swap(1, dbuf.at[core], dbuf.at[core]).start()
        for g, off in enumerate(groups):
            for k in range(0 if off else 1, chips):
                c_copy(g, off, chip, chip, k).wait_send()
        swap(1, dbuf.at[core], dbuf.at[1 - core]).wait()
        coef = jnp.concatenate(
            [dbuf[h, q : q + 1, :] for h in range(2) for q in range(half // LANES)], axis=1
        )
        coef_out[...] = coef
        wide = [
            jnp.broadcast_to(coef[:, q * LANES : (q + 1) * LANES], (8, LANES))
            for q in range(kk // LANES)
        ]

        def screen_step(i, c):
            for part in range(burst):
                at = pl.ds(pl.multiple_of((i * burst + part) * 8, 8), 8)
                value = basis[at, 0:LANES] * wide[0]
                for q in range(1, kk // LANES):
                    value = value + basis[at, q * LANES : (q + 1) * LANES] * wide[q]
                target[at, :] = value
            return c

        lax.fori_loop(0, rows // 8 // burst, screen_step, 0)
        if whole8 < rows:
            value = basis[whole8:rows, 0:LANES] * wide[0][0 : rows - whole8]
            for q in range(1, kk // LANES):
                value = value + (
                    basis[whole8:rows, q * LANES : (q + 1) * LANES] * wide[q][0 : rows - whole8]
                )
            target[whole8:rows, :] = value
        screen = jnp.sum(target[...], axis=1, keepdims=True)
        hot = ones3[:, 0:sp].astype(jnp.float32)
        for part, piece in enumerate(split3(screen)):
            place[:, part * sp : (part + 1) * sp] = (
                hot * piece.astype(jnp.float32)
            ).astype(jnp.bfloat16)
        placed = dot32(place[...], oned[...], 0, 0)
        split_out(placed[0:sp] + placed[sp : 2 * sp] + placed[2 * sp : 3 * sp])
        scatter_start(4, ebuf)
        ebuf[me] = stage[me]
        receive(4, ebuf)
        fbuf[me] = total(ebuf)
        gather_start(3, fbuf)
        drain(4, ebuf)
        receive(3, fbuf)
        return carry

    lax.fori_loop(0, ITERS, iteration, 0)
    drain(3, fbuf)
    join(fbuf, tec)
    for st in range(tec0_ref.shape[0]):
        tec_out[st] = tec[st : st + 1, 0:srcs]
    for j in range(tiles):
        lo = j * TILE
        width = min(TILE, base_n - lo)
        rr_out[0, :, lo : lo + width] = resr[j, :, 0:width]
        ri_out[0, :, lo : lo + width] = resi[j, :, 0:width]


def per_device(
    n, slots,
    measured_real, measured_imaginary, measured_weight, baseline_vectors, antenna_pairs,
    directions, direction_flux, channel_frequency, electron_content_start,
    pierce_station_direction, eigen_basis, eigen_weight,
):
    shard_slots, shard_channels, base_n = measured_real.shape
    assert shard_slots == 1 and shard_channels == 1
    stations, srcs = electron_content_start.shape[1:]
    rows, kk = eigen_basis.shape
    tiles = -(-base_n // TILE)
    drows = round_up(srcs, 16)
    dp = round_up(srcs, LANES)
    sp = round_up(stations, 64)
    cr = sp * (dp // LANES) // n
    rpad = round_up(rows + 1, 16)
    assert cr * n == sp * (dp // LANES) and n % 2 == 0 and kk % (2 * LANES) == 0
    groups = 1 + len({1 % slots, (slots - 1) % slots} - {0})

    own = lax.dynamic_slice_in_dim(
        pierce_station_direction[0], lax.axis_index("chan") * rows, rows, 0
    )
    f32, bf16 = jnp.float32, jnp.bfloat16
    vmem = pl.BlockSpec(memory_space=pltpu.VMEM)
    geo = (n, slots, tiles, base_n, srcs, drows, sp, dp, cr, rows, rpad, kk)
    tec_final, coefficients, res_re, res_im = pl.pallas_call(
        functools.partial(solve_kernel, geo),
        out_shape=(
            jax.ShapeDtypeStruct((stations, 1, srcs), f32),
            jax.ShapeDtypeStruct((1, kk), f32),
            jax.ShapeDtypeStruct((1, 1, base_n), f32),
            jax.ShapeDtypeStruct((1, 1, base_n), f32),
        ),
        in_specs=[vmem] * 7
        + [pl.BlockSpec(memory_space=pltpu.SMEM)]
        + [vmem] * 2
        + [pl.BlockSpec(memory_space=pl.ANY)]
        + [vmem],
        out_specs=(vmem,) * 4,
        scratch_shapes=[
            pltpu.VMEM((tiles, 1, TILE), f32),
            pltpu.VMEM((tiles, 1, TILE), f32),
            pltpu.VMEM((dp, 8), f32),
            pltpu.VMEM((8, round_up(rpad, LANES)), f32),
            pltpu.VMEM((tiles, 1, TILE), f32),
            pltpu.VMEM((tiles, 1, TILE), f32),
            pltpu.VMEM((tiles, 1, TILE), f32),
            pltpu.VMEM((tiles, drows, TILE), f32),
            pltpu.VMEM((tiles, 3 * sp, TILE), bf16),
            pltpu.VMEM((tiles, sp, TILE), bf16),
            pltpu.VMEM((drows, TILE), f32),
            pltpu.VMEM((drows, TILE), f32),
            pltpu.VMEM((drows, TILE), f32),
            pltpu.VMEM((drows, TILE), f32),
            pltpu.VMEM((drows, TILE), bf16),
            pltpu.VMEM((drows, TILE), bf16),
            pltpu.VMEM((sp, dp), f32),
            pltpu.VMEM((dp, 3 * sp), bf16),
            pltpu.VMEM((sp, dp), f32),
            pltpu.VMEM((cr, LANES), f32),
            pltpu.VMEM((rows, kk), f32),
            pltpu.VMEM((rpad, 3 * sp), bf16),
            pltpu.VMEM((rpad, dp), bf16),
            pltpu.VMEM((rpad, dp), f32),
            pltpu.VMEM((rpad, LANES), f32),
            pltpu.VMEM((rpad, 3 * sp), bf16),
            pltpu.VMEM((n, cr, LANES), f32),
            pltpu.VMEM((n, cr, LANES), f32),
            pltpu.VMEM((n, cr, LANES), f32),
            pltpu.VMEM((2, kk // 2 // LANES, LANES), f32),
            pltpu.VMEM((2, groups, n // 2, kk // 2 // LANES, LANES), f32),
            pltpu.VMEM((2, kk // 2 // LANES, LANES), f32),
            pltpu.VMEM((n, cr, LANES), f32),
            pltpu.VMEM((n, cr, LANES), f32),
            pltpu.VMEM((1, kk // 2 // LANES, LANES), f32),
            pltpu.SemaphoreType.DMA,
            pltpu.SemaphoreType.DMA((5, n)),
            pltpu.SemaphoreType.DMA((5, n)),
            pltpu.SemaphoreType.DMA((groups, n // 2)),
            pltpu.SemaphoreType.DMA((2, groups, n // 2)),
            pltpu.SemaphoreType.DMA((2,)),
            pltpu.SemaphoreType.DMA((2,)),
        ],
        compiler_params=pltpu.CompilerParams(
            collective_id=0, has_side_effects=True, vmem_limit_bytes=60 * 1024 * 1024
        ),
    )(
        measured_real, measured_imaginary, measured_weight,
        baseline_vectors.reshape(3, 1, base_n), antenna_pairs, directions,
        direction_flux, channel_frequency, electron_content_start.reshape(stations, 1, srcs),
        own.reshape(1, rows), eigen_basis, eigen_weight.reshape(1, kk),
    )
    return tec_final.reshape(1, stations, srcs), coefficients, res_re, res_im


def solution(mesh):
    in_specs = (
        P("slot", "chan", None),
        P("slot", "chan", None),
        P("slot", "chan", None),
        P("slot", None, None),
        P(),
        P(),
        P("chan", None),
        P("chan"),
        P("slot", None, None),
        P("slot", None),
        P("chan", None),
        P(),
    )
    out_specs = (
        P("slot", None, None),
        P("slot", None),
        P("slot", "chan", None),
        P("slot", "chan", None),
    )
    body = functools.partial(per_device, mesh.shape["chan"], mesh.shape["slot"])
    return jax.shard_map(body, mesh=mesh, in_specs=in_specs, out_specs=out_specs, check_vma=False)
```
